32 devices in a mesh: mem: 4 (over x, core), row: 4 (over z), col: 2 (over y).
Axes of the slice: x: 2, y: 2, z: 4, core: 2. Of those that a mesh axis runs over, the one named last changes fastest.
Arguments:
- fields: bfloat16 [16, 16, 64, 256], P('mem', 'row', 'col'), may hold values from -6 to 6
- norm_gain: float32 [256], replicated, may hold values from 0.5 to 1.5
- w_query: bfloat16 [256, 256], replicated, may hold values from -11 to 11
- w_key: bfloat16 [256, 256], replicated, may hold values from -6 to 6
- w_value: bfloat16 [256, 256], replicated, may hold values from -0.375 to 0.375
- w_out: bfloat16 [256, 256], replicated, may hold values from -0.375 to 0.375
- mix_kernel: float32 [3, 3, 256], replicated, may hold values from -1.5 to 1.5
- cotangent: bfloat16 [16, 16, 64, 256], P('mem', 'row', 'col'), may hold values from -6 to 6
Outputs:
- grad_fields: bfloat16 [16, 16, 64, 256], P('mem', 'row', 'col')
- grad_gain: float32 [256], replicated
- grad_query: float32 [256, 256], replicated
- grad_key: float32 [256, 256], replicated
- grad_value: float32 [256, 256], replicated
- grad_out: float32 [256, 256], replicated
- grad_kernel: float32 [3, 3, 256], replicated
The draws below stay inside these ranges and needn't reach their ends.
All inputs are finite; a program needn't handle non-finite values.
Results may differ from the reference program's by a relative error of at most 0.015.
The reference program's roundings to bfloat16 on the way count: a program that leaves them out, or rounds other values in their place, can miss the bound.
Values may be sent and summed in bfloat16 or wider, within the bound.
A program may use at most 64 MiB of HBM per device.

```python
import math
import jax
import jax.numpy as jnp
from jax import lax

D = 256
HEADS = 8
MEM_DEV = 4
MEMBERS = 16
NR = 16
NC = 64


def shared_basis(key):
    return jnp.clip(jax.random.normal(jax.random.fold_in(key, 11), (D, D), jnp.float32), -4.0, 4.0)


def draw_w_query(key, part):
    jitter = jnp.clip(jax.random.normal(jax.random.fold_in(key, 12), (D, D), jnp.float32), -4.0, 4.0)
    mixed = jitter
    return (mixed / math.sqrt(D)).astype(jnp.bfloat16)


def draw_w_key(key, part):
    basis = shared_basis(key)
    mixed = basis
    return (mixed / math.sqrt(D)).astype(jnp.bfloat16)


def block_scale(own_key, shape, pieces, smallest, high):
    def one(position, parts):
        heights = jax.random.uniform(jax.random.fold_in(jax.random.fold_in(own_key, 6), position), (parts,), jnp.float32, smallest / len(pieces), high / len(pieces))
        return jnp.repeat(jnp.exp(heights), shape[position] // parts).reshape((-1,) + (1,) * (len(shape) - position - 1))

    loudness = one(*pieces[0])
    for cut in pieces[1:]:
        loudness = loudness * one(*cut)
    return loudness


def normal_values(own_key, dims, scale, bound, split=(), kind=jnp.bfloat16):
    values = scale * jax.random.normal(own_key, dims, jnp.float32)
    if split:
        values = values * block_scale(own_key, dims, split, -0.22, 0.18)
    return jnp.clip(values, -bound, bound).astype(kind)


def setup_inputs(seed: int = 0) -> dict:
    key_list = jax.random.split(jax.random.key(seed), 9)
    fields = normal_values(key_list[0], (MEMBERS, NR, NC, D), 1.0, 6.0, ((0, 4), (1, 4), (2, 2)))
    norm_gain = jnp.clip(1.0 + 0.1 * jax.random.normal(key_list[1], (D,), jnp.float32), 0.5, 1.5)
    w_query = draw_w_query(jax.random.fold_in(key_list[8], 71), 0)
    w_key = draw_w_key(jax.random.fold_in(key_list[8], 71), 0)
    w_value = normal_values(key_list[4], (D, D), D ** -0.5, 0.375)
    w_out = normal_values(key_list[5], (D, D), D ** -0.5, 0.375)
    mix_kernel = normal_values(key_list[6], (3, 3, D), 0.3, 1.5, (), jnp.float32)
    cotangent = normal_values(key_list[7], (MEMBERS, NR, NC, D), 1.0, 6.0, ((0, 4), (1, 4), (2, 2)))
    return dict(fields=fields, norm_gain=norm_gain, w_query=w_query, w_key=w_key, w_value=w_value, w_out=w_out, mix_kernel=mix_kernel, cotangent=cotangent)


epsilon = 1e-06

def project(values, weight):
    shape = values.shape
    flat_in = values.reshape(-1, shape[-1])
    return jnp.dot(flat_in, weight, preferred_element_type=jnp.float32).reshape(shape[:-1] + (weight.shape[1],))

def reference(fields, norm_gain, w_query, w_key, w_value, w_out, mix_kernel, cotangent):
    members_all, grid_rows, grid_cols, model_width = fields.shape
    head_dim = model_width // HEADS
    score_scale = 1.0 / math.sqrt(head_dim)
    group_count = members_all // MEM_DEV
    padded_cot = jnp.pad(cotangent, ((0, 0), (1, 1), (1, 1), (0, 0)))
    summed = jnp.zeros(fields.shape, jnp.float32)
    for row_off in range(3):
        for col_off in range(3):
            summed = summed + mix_kernel[row_off, col_off] * padded_cot[:, 2 - row_off:2 - row_off + grid_rows, 2 - col_off:2 - col_off + grid_cols, :].astype(jnp.float32)
    grad_mixed_all = summed.astype(jnp.bfloat16)

    def attend_row(running, row_in):
        row_fields, row_grad_mixed, row_cot = row_in
        col_count = row_fields.shape[1]
        flat_in = row_fields.astype(jnp.float32)
        inv_rms = lax.rsqrt(lax.optimization_barrier(jnp.mean(flat_in * flat_in, axis=-1, keepdims=True)) + epsilon)
        normed = flat_in * inv_rms
        inputs = (normed * norm_gain).astype(jnp.bfloat16)
        queries = project(inputs, w_query).astype(jnp.bfloat16)
        key_proj = project(inputs, w_key).astype(jnp.bfloat16)
        value_proj = project(inputs, w_value).astype(jnp.bfloat16)
        head_shape = (members_all, col_count, HEADS, head_dim)
        query_heads = queries.reshape(head_shape).astype(jnp.float32)
        key_heads = key_proj.reshape(head_shape).astype(jnp.float32)
        value_heads = value_proj.reshape(head_shape).astype(jnp.float32)
        scores = jnp.einsum('mche,nche->chmn', query_heads, key_heads) * score_scale
        row_max = lax.optimization_barrier(jnp.max(scores, axis=-1, keepdims=True))
        lifted = jnp.exp(scores - row_max)
        attn_prob = lifted / lax.optimization_barrier(jnp.sum(lifted, axis=-1, keepdims=True))
        prob_b = attn_prob.astype(jnp.bfloat16).astype(jnp.float32)
        attended = jnp.einsum('chmn,nche->mche', prob_b, value_heads).astype(jnp.bfloat16)
        attended = attended.reshape(members_all, col_count, model_width)
        mixed_row = project(attended, w_out).astype(jnp.bfloat16)
        grad_att = project(row_grad_mixed, w_out.T).astype(jnp.bfloat16)
        grad_heads = grad_att.reshape(head_shape).astype(jnp.float32)
        grad_prob = jnp.einsum('mche,nche->chmn', grad_heads, value_heads)
        inner = lax.optimization_barrier(jnp.sum(attn_prob * grad_prob, axis=-1, keepdims=True))
        grad_score = (attn_prob * (grad_prob - inner) * score_scale).astype(jnp.bfloat16).astype(jnp.float32)
        grad_q = jnp.einsum('chmn,nche->mche', grad_score, key_heads).astype(jnp.bfloat16)
        score_groups = grad_score.reshape(col_count, HEADS, group_count, MEM_DEV, members_all)
        prob_groups = prob_b.reshape(col_count, HEADS, group_count, MEM_DEV, members_all)
        query_groups = query_heads.reshape(group_count, MEM_DEV, col_count, HEADS, head_dim)
        grad_groups = grad_heads.reshape(group_count, MEM_DEV, col_count, HEADS, head_dim)
        part_k = lax.optimization_barrier(jnp.einsum('chgmn,gmche->gnche', score_groups, query_groups).astype(jnp.bfloat16))
        part_v = lax.optimization_barrier(jnp.einsum('chgmn,gmche->gnche', prob_groups, grad_groups).astype(jnp.bfloat16))
        grad_k = lax.optimization_barrier(jnp.sum(part_k.astype(jnp.float32), axis=0)).astype(jnp.bfloat16)
        grad_v = lax.optimization_barrier(jnp.sum(part_v.astype(jnp.float32), axis=0)).astype(jnp.bfloat16)
        flat_shape = (members_all * col_count, model_width)
        grad_q2 = grad_q.reshape(flat_shape)
        grad_k2 = grad_k.reshape(flat_shape)
        grad_v2 = grad_v.reshape(flat_shape)
        inputs2 = inputs.reshape(flat_shape)
        grad_in = jnp.dot(grad_q2, w_query.T, preferred_element_type=jnp.float32) + jnp.dot(grad_k2, w_key.T, preferred_element_type=jnp.float32) + jnp.dot(grad_v2, w_value.T, preferred_element_type=jnp.float32)
        normed2 = normed.reshape(flat_shape)
        grad_normed = grad_in * norm_gain
        inv2 = inv_rms.reshape(-1, 1)
        grad_row = row_cot.reshape(flat_shape).astype(jnp.float32) + inv2 * (grad_normed - normed2 * lax.optimization_barrier(jnp.mean(grad_normed * normed2, axis=-1, keepdims=True)))
        acc_q, acc_k, acc_v, acc_out, acc_gain = running
        acc_q = acc_q + jnp.dot(inputs2.T, grad_q2, preferred_element_type=jnp.float32)
        acc_k = acc_k + jnp.dot(inputs2.T, grad_k2, preferred_element_type=jnp.float32)
        acc_v = acc_v + jnp.dot(inputs2.T, grad_v2, preferred_element_type=jnp.float32)
        acc_out = acc_out + jnp.dot(attended.reshape(flat_shape).T, row_grad_mixed.reshape(flat_shape), preferred_element_type=jnp.float32)
        acc_gain = acc_gain + lax.optimization_barrier(jnp.sum(grad_in * normed2, axis=0))
        outputs = (mixed_row, grad_row.astype(jnp.bfloat16).reshape(members_all, col_count, model_width))
        return ((acc_q, acc_k, acc_v, acc_out, acc_gain), outputs)
    square = jnp.zeros((model_width, model_width), jnp.float32)
    start = (square, square, square, square, jnp.zeros((model_width,), jnp.float32))
    row_inputs = (jnp.moveaxis(fields, 1, 0), jnp.moveaxis(grad_mixed_all, 1, 0), jnp.moveaxis(cotangent, 1, 0))
    running, outputs = lax.scan(attend_row, start, row_inputs)
    mixed_all = jnp.moveaxis(outputs[0], 0, 1)
    grad_fields = jnp.moveaxis(outputs[1], 0, 1)
    scale_all = 1.0 / math.sqrt(members_all * grid_rows * grid_cols)
    kernel_terms = []
    padded_mixed = jnp.pad(mixed_all, ((0, 0), (1, 1), (1, 1), (0, 0)))
    for row_off in range(3):
        for col_off in range(3):
            shifted = padded_mixed[:, row_off:row_off + grid_rows, col_off:col_off + grid_cols, :].astype(jnp.float32)
            kernel_terms.append(lax.optimization_barrier(jnp.sum(shifted * cotangent.astype(jnp.float32), axis=(0, 1, 2))))
    grad_kernel = jnp.stack(kernel_terms).reshape(3, 3, model_width) * scale_all
    acc_q, acc_k, acc_v, acc_out, acc_gain = running
    return (grad_fields, acc_gain * scale_all, acc_q * scale_all, acc_k * scale_all, acc_v * scale_all, acc_out * scale_all, grad_kernel)
```

```python
import functools
import math

import jax
import jax.numpy as jnp
from jax import lax
from jax.experimental import pallas as pl
from jax.experimental.pallas import tpu as pltpu
from jax.sharding import PartitionSpec as P

HEADS = 8
SUB = 8
BLOCK = 16
EDGE = 8

epsilon = 1e-06
F32 = jnp.float32
BF16 = jnp.bfloat16
MESH = pl.DeviceIdType.MESH
VMEM_SPEC = pl.BlockSpec(memory_space=pltpu.VMEM)
HBM_SPEC = pl.BlockSpec(memory_space=pltpu.HBM)
NEAR = [(dr, dc) for dr in (-1, 0, 1) for dc in (-1, 0, 1) if (dr, dc) != (0, 0)]


def dot_nn(a, b):
    return lax.dot_general(a, b, (((1,), (0,)), ((), ())), preferred_element_type=F32)


def dot_nt(a, b):
    return lax.dot_general(a, b, (((1,), (1,)), ((), ())), preferred_element_type=F32)


def one_hot(size, target):
    row = lax.broadcasted_iota(jnp.int32, (size, size), 0)
    col = lax.broadcasted_iota(jnp.int32, (size, size), 1)
    return jnp.where(target(row) == col, 1.0, 0.0).astype(BF16)


def cell_first(members):
    size = members * BLOCK
    there = one_hot(size, lambda i: lax.rem(i, members) * BLOCK + lax.div(i, members))
    back = one_hot(size, lambda i: lax.rem(i, BLOCK) * members + lax.div(i, BLOCK))
    return there, back


def cell_masks(members):
    tokens = SUB * members
    lane = lax.div(lax.broadcasted_iota(jnp.int32, (members, tokens), 1), members)
    own = [lane == c for c in range(SUB)]
    return own, [jnp.where(o, 1.0, 0.0).astype(BF16) for o in own]


def own_cells(left, right_t, own):
    tokens, width = left.shape
    members = tokens // SUB
    dim = width // HEADS
    zeros = jnp.zeros((dim, tokens), right_t.dtype)
    heads = []
    for h in range(0, HEADS, 2):
        pair = [
            jnp.concatenate(
                [right_t[k * dim : (k + 1) * dim] if k == p else zeros for k in range(HEADS)], axis=0
            )
            for p in (h, h + 1)
        ]
        both = dot_nn(left, jnp.concatenate(pair, axis=1))
        for i in range(2):
            full = both[:, i * tokens : (i + 1) * tokens]
            picked = full[:members]
            for c in range(1, SUB):
                picked = jnp.where(own[c], full[c * members : (c + 1) * members], picked)
            heads.append(picked)
    return jnp.stack(heads)


def spread(packed, mask):
    return jnp.concatenate([packed * m for m in mask], axis=0)


def softmax_group(keys, q_t, own):
    dim = keys.shape[1] // HEADS
    scores = own_cells(keys, q_t, own) * (1.0 / math.sqrt(dim))
    lifted = jnp.exp(scores - jnp.max(scores, axis=1, keepdims=True))
    return lifted * (1.0 / jnp.sum(lifted, axis=1, keepdims=True))


def attend_group(prob, v_t, mask):
    dim = v_t.shape[0] // HEADS
    return jnp.concatenate(
        [
            dot_nn(v_t[h * dim : (h + 1) * dim], spread(prob[h].astype(BF16), mask))
            for h in range(HEADS)
        ],
        axis=0,
    ).astype(BF16)


def back_group(prob, vals, q_t, ga_t, k_t, own, mask):
    dim = vals.shape[1] // HEADS
    grad_prob = own_cells(vals, ga_t, own)
    inner = jnp.sum(prob * grad_prob, axis=1, keepdims=True)
    grad_score = prob * (grad_prob - inner) * (1.0 / math.sqrt(dim))
    outs = ([], [], [])
    for h in range(HEADS):
        hs = slice(h * dim, (h + 1) * dim)
        gs = spread(grad_score[h].astype(BF16), mask)
        pb = spread(prob[h].astype(BF16), mask)
        outs[0].append(dot_nn(k_t[hs], gs))
        outs[1].append(dot_nt(q_t[hs], gs))
        outs[2].append(dot_nt(ga_t[hs], pb))
    return tuple(jnp.concatenate(o, axis=0).astype(BF16) for o in outs)


def groups_of(tokens, members):
    size = SUB * members
    return [slice(i, i + size) for i in range(0, tokens, size)]


def forward_block(x, gain, wq_t, wk_t, wv_t, wk, wv, wo, there, back, eye, own, mask):
    tokens = x.shape[0]
    members = tokens // BLOCK
    inv = lax.rsqrt(jnp.mean(x * x, axis=-1, keepdims=True) + epsilon)
    normed = x * inv
    inputs = dot_nn(there, (normed * gain).astype(BF16)).astype(BF16)
    keys = dot_nn(inputs, wk).astype(BF16)
    vals = dot_nn(inputs, wv).astype(BF16)
    q_t = dot_nt(wq_t, inputs).astype(BF16)
    k_t = dot_nt(wk_t, inputs).astype(BF16)
    v_t = dot_nt(wv_t, inputs).astype(BF16)
    in_t = dot_nt(eye, inputs).astype(BF16)
    probs, parts = [], []
    for s in groups_of(tokens, members):
        prob = softmax_group(keys[s], q_t[:, s], own)
        probs.append(prob)
        parts.append(attend_group(prob, v_t[:, s], mask))
    att_t = jnp.concatenate(parts, axis=1)
    mixed = dot_nn(dot_nt(back, att_t).astype(BF16), wo).astype(BF16)
    return mixed, (inv, normed, vals, q_t, k_t, in_t, att_t, probs)


def backward_block(gm, saved, wo, there, own, mask):
    inv, normed, vals, q_t, k_t, in_t, att_t, probs = saved
    tokens = gm.shape[0]
    gm = dot_nn(there, gm).astype(BF16)
    ga_t = dot_nt(wo, gm).astype(BF16)
    parts = [
        back_group(prob, vals[s], q_t[:, s], ga_t[:, s], k_t[:, s], own, mask)
        for s, prob in zip(groups_of(tokens, tokens // BLOCK), probs)
    ]
    return (gm,) + tuple(jnp.concatenate(p, axis=1) for p in zip(*parts))


def input_block(gq_t, gk_t, gv_t, saved, gain, wq, wk, wv, back):
    inv, normed = saved[:2]
    rows = [dot_nt(back, g).astype(BF16) for g in (gq_t, gk_t, gv_t)]
    grad_in = dot_nt(rows[0], wq) + dot_nt(rows[1], wk) + dot_nt(rows[2], wv)
    grad_normed = grad_in * gain
    corr = inv * (grad_normed - normed * jnp.mean(grad_normed * normed, axis=-1, keepdims=True))
    return corr.astype(BF16), jnp.sum(grad_in * normed, axis=0, keepdims=True)


def push(src, dst, send_sem, recv_sem, peer):
    return pltpu.make_async_remote_copy(
        src_ref=src, dst_ref=dst, send_sem=send_sem, recv_sem=recv_sem,
        device_id=peer, device_id_type=MESH,
    )


def main_kernel(
    sizes, scale,
    f_hbm, cot_hbm, gain_hbm, wq_hbm, wk_hbm, wv_hbm, wo_hbm, taps_hbm,
    gf_ref, out_ref, small_ref,
    cot, gain_v, wq_v, wk_v, wv_v, wo_v, taps, f_got, gm_src, gm_got, mx_src, mx_got,
    co_src, co_got, row_halo, edges, col_halo, pad,
    g, a_src, a_dst, acc1, b_src, b_dst, c_src, c_dst, ga, s_a, s_b, s_c,
    load, near_send, near_recv, f_send, f_recv, gm_send, gm_recv, mx_send, mx_recv,
    co_send, co_recv, a_send, a_recv, b_send, b_recv, c_send, c_recv, z_send, z_recv,
    p_send, p_recv, g_send, g_recv,
    sa_send, sa_recv, sb_send, sb_recv, sc_send, sc_recv,
):
    count, grid_rows, grid_cols = sizes
    members, rows, cols, width = cot.shape
    cells = f_got.shape[2]
    planes = count // 2 * grid_cols
    unit = g.shape[3]
    mem, row, col = (lax.axis_index(a) for a in ("mem", "row", "col"))
    at = (row, col)
    core, chip = lax.rem(mem, 2), lax.div(mem, 2)
    other = 1 - core
    partner = (mem + 1 - 2 * core, row, col)
    me_p = chip * grid_cols + col

    def plane_peer(p):
        return (lax.div(p, grid_cols) * 2 + core, row, lax.rem(p, grid_cols))

    mem_others = [lax.rem(mem + k, count) for k in range(1, count)]
    plane_others = [lax.rem(me_p + k, planes) for k in range(1, planes)]
    step_z = 1 - 2 * lax.div(row * 2, grid_rows)
    row_others = [
        lax.rem(row + step_z * k + grid_rows, grid_rows) for k in range(1, grid_rows)
    ]

    local = [
        pltpu.make_async_copy(cot_hbm, cot, load.at[0]),
        pltpu.make_async_copy(taps_hbm, taps, load.at[1]),
        pltpu.make_async_copy(wq_hbm, wq_v, load.at[2]),
        pltpu.make_async_copy(wk_hbm, wk_v, load.at[3]),
        pltpu.make_async_copy(wv_hbm, wv_v, load.at[4]),
        pltpu.make_async_copy(wo_hbm, wo_v, load.at[5]),
        pltpu.make_async_copy(gain_hbm, gain_v, load.at[6]),
        pltpu.make_async_copy(f_hbm.at[:, mem], f_got.at[mem], load.at[7]),
    ]
    for copy in local:
        copy.start()

    def exists(step):
        tests = [
            (at[i] > 0) if step[i] < 0 else (at[i] < (grid_rows, grid_cols)[i] - 1)
            for i in range(2)
            if step[i]
        ]
        return functools.reduce(jnp.logical_and, tests)

    def neighbour(step):
        return (mem, row + step[0], col + step[1])

    barrier = pltpu.get_barrier_semaphore()

    def greet(peer):
        pl.semaphore_signal(barrier, inc=1, device_id=peer, device_id_type=MESH)

    greeted = 0
    for r in row_others:
        greet((mem, r, col))
        greeted += 1
    for o in mem_others:
        greet((o, row, col))
        greeted += 1
    for k in range(count // 2):
        for c in range(1, grid_cols):
            there_chip = lax.rem(chip + k, count // 2)
            greet((there_chip * 2 + core, row, lax.rem(col + c, grid_cols)))
            greeted += 1
    diagonal = [step for step in NEAR if step[0] and step[1]]
    for step in diagonal:
        @pl.when(exists(step))
        def _():
            greet(neighbour(step))
    present = sum(exists(step).astype(jnp.int32) for step in diagonal)

    def outgoing(step):
        dr, dc = step
        if dc == 0:
            return cot.at[:, 0 if dr < 0 else rows - 1]
        side = edges.at[0 if dc < 0 else 1]
        return side if dr == 0 else side.at[0 if dr < 0 else rows - 1]

    def landing(step):
        dr, dc = step
        if dc == 0:
            return row_halo.at[0 if dr < 0 else 1]
        side = col_halo.at[0 if dc < 0 else 1]
        return side.at[pl.ds(1, rows)] if dr == 0 else side.at[0 if dr < 0 else rows + 1]

    def halo_copy(i):
        step = NEAR[i]
        back_i = len(NEAR) - 1 - i
        return push(
            outgoing(step), landing(NEAR[back_i]), near_send.at[i], near_recv.at[back_i],
            neighbour(step),
        )

    local[0].wait()
    pad[:, 1 : rows + 1, EDGE : EDGE + cols, :] = cot[...].astype(F32)
    for m in range(members):
        for r in range(rows):
            edges[0, r, m : m + 1] = cot[m, r, 0:BLOCK].astype(F32)[:1]
            edges[1, r, m : m + 1] = cot[m, r, cols - BLOCK : cols].astype(F32)[BLOCK - 1 :]
    for i in range(len(NEAR)):
        @pl.when(jnp.logical_not(exists(NEAR[i])))
        def _():
            there_ref = landing(NEAR[i])
            there_ref[...] = jnp.zeros(there_ref.shape, there_ref.dtype)

    pl.semaphore_wait(barrier, present + greeted)

    for i in range(len(NEAR)):
        @pl.when(exists(NEAR[i]))
        def _():
            halo_copy(i).start()
    sent = []

    def start(copy):
        copy.start()
        sent.append(copy)

    for o in mem_others:
        start(push(f_hbm.at[:, o], f_got.at[mem], f_send.at[o], f_recv.at[mem], (o, *at)))

    for copy in local[1:]:
        copy.wait()
    eye = one_hot(width, lambda i: i)
    there, back = cell_first(count * members)
    own, mask = cell_masks(count * members)
    wq, wk, wv, wo = (w[...] for w in (wq_v, wk_v, wv_v, wo_v))
    wq_t, wk_t, wv_t = (dot_nt(eye, w).astype(BF16) for w in (wq, wk, wv))
    gain = gain_v[...]
    taps9 = [[taps[i, j : j + 1, :] for j in range(3)] for i in range(3)]

    for i in range(len(NEAR)):
        @pl.when(exists(NEAR[i]))
        def _():
            there_ref = landing(NEAR[i])
            push(
                there_ref, there_ref, near_send.at[i], near_recv.at[i], neighbour(NEAR[i])
            ).wait_recv()
    pad[:, 0, EDGE : EDGE + cols, :] = row_halo[0].astype(F32)
    pad[:, rows + 1, EDGE : EDGE + cols, :] = row_halo[1].astype(F32)
    for side, place in ((0, EDGE - 1), (1, EDGE + cols)):
        for r in range(rows + 2):
            column = col_halo[side, r]
            for m in range(members):
                pad[m, r, place : place + 1, :] = column[m : m + 1]

    seg = min(cells, cols)

    def segments(j):
        for s in range(cells // seg):
            cell = j * cells + s * seg
            yield s * seg, cell // cols, cell % cols

    for j in range(count):
        for first, r, c in segments(j):
            for m in range(members):
                wins = [pad[m, 2 - i + r, c : c + seg + 2 * EDGE, :] for i in range(3)]
                cols3 = [sum(taps9[i][k] * wins[i] for i in range(3)) for k in range(3)]
                summed = sum(
                    cols3[k][EDGE + 1 - k : EDGE + 1 - k + seg] for k in range(3)
                )
                gm_src[m, j, first : first + seg, :] = summed.astype(BF16)

        @pl.when(mem != j)
        def _():
            push(gm_src.at[:, j], gm_got.at[mem], gm_send.at[j], gm_recv.at[mem], (j, *at)).start()

        @pl.when(mem == j)
        def _():
            gm_got[j] = gm_src[:, j]

    for o in mem_others:
        push(f_hbm.at[:, o], f_got.at[o], f_send.at[o], f_recv.at[o], (o, *at)).wait_recv()
    blocks = [slice(i, i + BLOCK) for i in range(0, cells, BLOCK)]
    tokens = count * members * BLOCK
    saved = []
    for b in blocks:
        x = f_got[:, :, b, :].reshape(tokens, width).astype(F32)
        mixed, keep = forward_block(
            x, gain, wq_t, wk_t, wv_t, wk, wv, wo, there, back, eye, own, mask
        )
        mx_src[:, :, b, :] = mixed.reshape(count, members, BLOCK, width)
        saved.append(keep)
    for o in mem_others:
        start(push(mx_src.at[o], mx_got.at[:, mem], mx_send.at[o], mx_recv.at[mem], (o, *at)))
    mx_got[:, mem] = mx_src[mem]

    for o in mem_others:
        push(gm_src.at[:, o], gm_got.at[o], gm_send.at[o], gm_recv.at[o], (o, *at)).wait_recv()
    grads = [
        backward_block(gm_got[:, :, b, :].reshape(tokens, width), keep, wo, there, own, mask)
        for b, keep in zip(blocks, saved)
    ]
    gms = jnp.concatenate([x[0] for x in grads], axis=0)
    in_t = jnp.concatenate([keep[5] for keep in saved], axis=1)
    att_t = jnp.concatenate([keep[6] for keep in saved], axis=1)
    wholes = [
        dot_nt(in_t, jnp.concatenate([x[i] for x in grads], axis=1)) for i in (1, 2, 3)
    ] + [dot_nn(att_t, gms)]
    for i, value in enumerate(wholes):
        for k in range(width // unit):
            flat = i * (width // unit) + k
            half, rest = divmod(flat, planes * grid_rows)
            g[half, rest // grid_rows, rest % grid_rows] = value[k * unit : (k + 1) * unit]

    a_src[...] = g[other].astype(BF16)
    first_copy = push(a_src, a_dst, a_send, a_recv, partner)
    first_copy.start()
    gain_sum = jnp.zeros((1, width), F32)
    for b, keep, x in zip(blocks, saved, grads):
        corr, part = input_block(*x[1:], keep, gain, wq, wk, wv, back)
        co_src[:, :, b, :] = corr.reshape(count, members, BLOCK, width)
        gain_sum = gain_sum + part
    first_copy.wait()
    acc1[...] = g[core] + a_dst[...].astype(F32)
    b_src[...] = acc1[...].astype(BF16)
    turns = row_others[::-1] + [row]
    for r in turns:
        for p in plane_others:
            start(push(
                b_src.at[p, r], b_dst.at[me_p, r], b_send.at[p, r], b_recv.at[me_p, r],
                plane_peer(p),
            ))
    for o in mem_others:
        start(push(co_src.at[o], co_got.at[:, mem], co_send.at[o], co_recv.at[mem], (o, *at)))
    co_got[:, mem] = co_src[mem]

    for o in mem_others:
        push(mx_src.at[o], mx_got.at[:, o], mx_send.at[o], mx_recv.at[o], (o, *at)).wait_recv()
    kernel_sum = [[jnp.zeros((8, width), F32) for _ in range(3)] for _ in range(3)]
    for j in range(count):
        for first, r, c in segments(j):
            for m in range(members):
                mx = mx_got[m, j, first : first + seg, :].astype(F32)
                for k in range(3):
                    ahead = EDGE + 1 - k
                    wide = jnp.concatenate(
                        [
                            jnp.zeros((ahead, width), F32), mx,
                            jnp.zeros((2 * EDGE - ahead, width), F32),
                        ],
                        axis=0,
                    )
                    for i in range(3):
                        win = pad[m, 2 - i + r, c : c + seg + 2 * EDGE, :]
                        product = (wide * win).reshape(-1, 8, width)
                        kernel_sum[i][k] = kernel_sum[i][k] + jnp.sum(product, axis=0)
    s_a[core] = jnp.concatenate(
        [gain_sum]
        + [jnp.sum(kernel_sum[i][k], axis=0, keepdims=True) for i in range(3) for k in range(3)]
        + [jnp.zeros((6, width), F32)],
        axis=0,
    )
    start(push(s_a.at[core], s_a.at[core], sa_send, sa_recv, partner))

    for r in turns:
        for p in plane_others:
            push(
                b_src.at[p, r], b_dst.at[p, r], b_send.at[p, r], b_recv.at[p, r], plane_peer(p)
            ).wait_recv()
        whole = acc1[me_p, r]
        for p in plane_others:
            whole = whole + b_dst[p, r].astype(F32)
        if r is not row:
            c_src[r] = whole.astype(BF16)
            start(push(c_src.at[r], c_dst.at[row], c_send.at[r], c_recv.at[row], (mem, r, col)))
    push(s_a.at[other], s_a.at[other], sa_send, sa_recv, partner).wait_recv()
    s_b[me_p] = s_a[0] + s_a[1]
    for p in plane_others:
        start(push(
            s_b.at[me_p], s_b.at[me_p], sb_send.at[p], sb_recv.at[me_p], plane_peer(p)
        ))
    for r in row_others:
        push(c_src.at[r], c_dst.at[r], c_send.at[r], c_recv.at[r], (mem, r, col)).wait_recv()
        whole = whole + c_dst[r].astype(F32)
    ga[core, me_p, row] = (whole * scale).astype(BF16)

    for r in row_others:
        piece = ga.at[core, me_p, row]
        start(push(piece, piece, z_send.at[r], z_recv.at[row], (mem, r, col)))

    def to_partner(p, r):
        piece = ga.at[core, p, r]
        start(push(piece, piece, g_send.at[p, r], g_recv.at[p, r], partner))
        out_ref[core, p, r] = ga[core, p, r].astype(F32)

    def to_plane(r):
        piece = ga.at[core, me_p, r]
        for p in plane_others:
            start(push(piece, piece, p_send.at[p, r], p_recv.at[me_p, r], plane_peer(p)))
        to_partner(me_p, r)

    def from_plane(r):
        for p in plane_others:
            piece = ga.at[core, p, r]
            push(piece, piece, p_send.at[p, r], p_recv.at[p, r], plane_peer(p)).wait_recv()
            to_partner(p, r)

    to_plane(row)
    for p in plane_others:
        push(s_b.at[p], s_b.at[p], sb_send.at[p], sb_recv.at[p], plane_peer(p)).wait_recv()
    s_c[row] = sum(s_b[p] for p in range(planes))
    for r in row_others:
        start(push(s_c.at[row], s_c.at[row], sc_send.at[r], sc_recv.at[row], (mem, r, col)))
    for o in mem_others:
        push(co_src.at[o], co_got.at[:, o], co_send.at[o], co_recv.at[o], (o, *at)).wait_recv()
    gf_ref[...] = (
        cot[...].astype(F32) + co_got[...].reshape(cot.shape).astype(F32)
    ).astype(BF16)

    before = row
    for r in row_others:
        piece = ga.at[core, me_p, r]
        push(piece, piece, z_send.at[r], z_recv.at[r], (mem, r, col)).wait_recv()
        to_plane(r)
        from_plane(before)
        before = r
    from_plane(before)
    for r in row_others:
        push(s_c.at[r], s_c.at[r], sc_send.at[r], sc_recv.at[r], (mem, r, col)).wait_recv()
    small_ref[...] = sum(s_c[r] for r in range(grid_rows)) * scale
    for r in [row] + row_others:
        for p in [me_p] + plane_others:
            piece = ga.at[other, p, r]
            push(piece, piece, g_send.at[p, r], g_recv.at[p, r], partner).wait_recv()
            out_ref[other, p, r] = ga[other, p, r].astype(F32)

    for copy in sent:
        copy.wait_send()
    for i in range(len(NEAR)):
        @pl.when(exists(NEAR[i]))
        def _():
            halo_copy(i).wait_send()
    for j in range(count):
        @pl.when(mem != j)
        def _():
            push(
                gm_src.at[:, j], gm_got.at[mem], gm_send.at[j], gm_recv.at[mem], (j, *at)
            ).wait_send()


def output_kernel(
    gf_in, out_in, small_in, gf, gain, gq, gk, gv, go, taps, taps_v, sems,
):
    copies = [
        pltpu.make_async_copy(out_in.at[i], ref, sems.at[i]) for i, ref in enumerate((gq, gk, gv, go))
    ]
    copies.append(pltpu.make_async_copy(gf_in, gf, sems.at[4]))
    copies.append(pltpu.make_async_copy(small_in.at[pl.ds(0, 1)], gain, sems.at[5]))
    for copy in copies:
        copy.start()
    for i in range(3):
        taps_v[i] = small_in[1 + 3 * i : 4 + 3 * i, :]
    last = pltpu.make_async_copy(taps_v, taps, sems.at[6])
    last.start()
    for copy in copies:
        copy.wait()
    last.wait()


def local(fields, norm_gain, w_query, w_key, w_value, w_out, mix_kernel, cotangent):
    members, rows, cols, width = fields.shape
    count, grid_rows, grid_cols = (lax.axis_size(a) for a in ("mem", "row", "col"))
    cells = rows * cols // count
    planes = count // 2 * grid_cols
    height = 4 * width
    unit = height // (2 * planes * grid_rows)
    tokens = math.prod(fields.shape[:3]) * count * grid_rows * grid_cols
    sems = pltpu.SemaphoreType.DMA
    vmem = pltpu.VMEM
    split = (members, count, cells, width)
    got = (count, members, cells, width)
    square = vmem((width, width), BF16)
    half = (planes, grid_rows, unit, width)
    line = (grid_rows, unit, width)
    small = (16, width)

    def pair(shape):
        return [sems(shape), sems(shape)]

    gf, out, small_sum = pl.pallas_call(
        functools.partial(
            main_kernel, (count, grid_rows, grid_cols), 1.0 / math.sqrt(tokens)
        ),
        out_shape=(
            jax.ShapeDtypeStruct(fields.shape, BF16),
            jax.ShapeDtypeStruct((2,) + half, F32),
            jax.ShapeDtypeStruct(small, F32),
        ),
        in_specs=[HBM_SPEC] * 8,
        out_specs=(VMEM_SPEC,) * 3,
        scratch_shapes=[
            vmem(fields.shape, BF16), vmem((1, width), F32), square, square, square, square,
            vmem((3, 3, width), F32),
            vmem(got, BF16), vmem(split, BF16), vmem(got, BF16), vmem(got, BF16), vmem(split, BF16),
            vmem(got, BF16), vmem(split, BF16),
            vmem((2, members, cols, width), BF16),
            vmem((2, rows, members, width), F32), vmem((2, rows + 2, members, width), F32),
            vmem((members, rows + 2, cols + 2 * EDGE, width), F32),
            vmem((2,) + half, F32), vmem(half, BF16), vmem(half, BF16), vmem(half, F32),
            vmem(half, BF16), vmem(half, BF16), vmem(line, BF16), vmem(line, BF16),
            vmem((2,) + half, BF16),
            vmem((2,) + small, F32), vmem((planes,) + small, F32), vmem((grid_rows,) + small, F32),
            sems((8,)), *pair((len(NEAR),)),
            *pair((count,)), *pair((count,)), *pair((count,)), *pair((count,)),
            *pair(()), *pair((planes, grid_rows)), *pair((grid_rows,)), *pair((grid_rows,)),
            *pair((planes, grid_rows)), *pair((planes, grid_rows)),
            *pair(()), *pair((planes,)), *pair((grid_rows,)),
        ],
        compiler_params=pltpu.CompilerParams(
            collective_id=1, has_side_effects=True, vmem_limit_bytes=56 * 2**20
        ),
    )(
        fields.reshape(split), cotangent, norm_gain.reshape(1, -1),
        w_query, w_key, w_value, w_out, mix_kernel,
    )
    square32 = jax.ShapeDtypeStruct((width, width), F32)
    gf, gain, gq, gk, gv, go, taps = pl.pallas_call(
        output_kernel,
        out_shape=(
            jax.ShapeDtypeStruct(fields.shape, BF16), jax.ShapeDtypeStruct((1, width), F32),
            square32, square32, square32, square32,
            jax.ShapeDtypeStruct((3, 3, width), F32),
        ),
        in_specs=[VMEM_SPEC] * 3,
        out_specs=(HBM_SPEC,) * 7,
        scratch_shapes=[vmem((3, 3, width), F32), sems((7,))],
        compiler_params=pltpu.CompilerParams(vmem_limit_bytes=16 * 2**20),
    )(gf, out.reshape(4, width, width), small_sum)
    return (gf, gain.reshape(-1), gq, gk, gv, go, taps)


def solution(mesh):
    tile = P("mem", "row", "col", None)
    in_specs = (tile, P(), P(), P(), P(), P(), P(), tile)
    out_specs = (tile, P(), P(), P(), P(), P(), P())
    return jax.shard_map(local, mesh=mesh, in_specs=in_specs, out_specs=out_specs, check_vma=False)
```

```python
import functools
import math

import jax
import jax.numpy as jnp
from jax import lax
from jax.experimental import pallas as pl
from jax.experimental.pallas import tpu as pltpu
from jax.sharding import PartitionSpec as P

HEADS = 8
SUB = 8
BLOCK = 16
EDGE = 8

epsilon = 1e-06
F32 = jnp.float32
BF16 = jnp.bfloat16
MESH = pl.DeviceIdType.MESH
VMEM_SPEC = pl.BlockSpec(memory_space=pltpu.VMEM)
HBM_SPEC = pl.BlockSpec(memory_space=pltpu.HBM)
NEAR = [(dr, dc) for dr in (-1, 0, 1) for dc in (-1, 0, 1) if (dr, dc) != (0, 0)]


def dot_nn(a, b):
    return lax.dot_general(a, b, (((1,), (0,)), ((), ())), preferred_element_type=F32)


def dot_nt(a, b):
    return lax.dot_general(a, b, (((1,), (1,)), ((), ())), preferred_element_type=F32)


def one_hot(size, target):
    row = lax.broadcasted_iota(jnp.int32, (size, size), 0)
    col = lax.broadcasted_iota(jnp.int32, (size, size), 1)
    return jnp.where(target(row) == col, 1.0, 0.0).astype(BF16)


def cell_first(members):
    size = members * BLOCK
    there = one_hot(size, lambda i: lax.rem(i, members) * BLOCK + lax.div(i, members))
    back = one_hot(size, lambda i: lax.rem(i, BLOCK) * members + lax.div(i, BLOCK))
    return there, back


def cell_masks(members):
    tokens = SUB * members
    lane = lax.div(lax.broadcasted_iota(jnp.int32, (members, tokens), 1), members)
    own = [lane == c for c in range(SUB)]
    return own, [jnp.where(o, 1.0, 0.0).astype(BF16) for o in own]


def own_cells(left, right_t, own):
    tokens, width = left.shape
    members = tokens // SUB
    dim = width // HEADS
    zeros = jnp.zeros((dim, tokens), right_t.dtype)
    heads = []
    for h in range(0, HEADS, 2):
        pair = [
            jnp.concatenate(
                [right_t[k * dim : (k + 1) * dim] if k == p else zeros for k in range(HEADS)], axis=0
            )
            for p in (h, h + 1)
        ]
        both = dot_nn(left, jnp.concatenate(pair, axis=1))
        for i in range(2):
            full = both[:, i * tokens : (i + 1) * tokens]
            picked = full[:members]
            for c in range(1, SUB):
                picked = jnp.where(own[c], full[c * members : (c + 1) * members], picked)
            heads.append(picked)
    return jnp.stack(heads)


def spread(packed, mask):
    return jnp.concatenate([packed * m for m in mask], axis=0)


def softmax_group(keys, q_t, own):
    dim = keys.shape[1] // HEADS
    scores = own_cells(keys, q_t, own) * (1.0 / math.sqrt(dim))
    lifted = jnp.exp(scores - jnp.max(scores, axis=1, keepdims=True))
    return lifted * (1.0 / jnp.sum(lifted, axis=1, keepdims=True))


def attend_group(prob, v_t, mask):
    dim = v_t.shape[0] // HEADS
    return jnp.concatenate(
        [
            dot_nn(v_t[h * dim : (h + 1) * dim], spread(prob[h].astype(BF16), mask))
            for h in range(HEADS)
        ],
        axis=0,
    ).astype(BF16)


def back_group(prob, vals, q_t, ga_t, k_t, own, mask):
    dim = vals.shape[1] // HEADS
    grad_prob = own_cells(vals, ga_t, own)
    inner = jnp.sum(prob * grad_prob, axis=1, keepdims=True)
    grad_score = prob * (grad_prob - inner) * (1.0 / math.sqrt(dim))
    outs = ([], [], [])
    for h in range(HEADS):
        hs = slice(h * dim, (h + 1) * dim)
        gs = spread(grad_score[h].astype(BF16), mask)
        pb = spread(prob[h].astype(BF16), mask)
        outs[0].append(dot_nn(k_t[hs], gs))
        outs[1].append(dot_nt(q_t[hs], gs))
        outs[2].append(dot_nt(ga_t[hs], pb))
    return tuple(jnp.concatenate(o, axis=0).astype(BF16) for o in outs)


def groups_of(tokens, members):
    size = SUB * members
    return [slice(i, i + size) for i in range(0, tokens, size)]


def forward_block(x, gain, wq_t, wk_t, wv_t, wk, wv, wo, there, back, eye, own, mask):
    tokens = x.shape[0]
    members = tokens // BLOCK
    inv = lax.rsqrt(jnp.mean(x * x, axis=-1, keepdims=True) + epsilon)
    normed = x * inv
    inputs = dot_nn(there, (normed * gain).astype(BF16)).astype(BF16)
    keys = dot_nn(inputs, wk).astype(BF16)
    vals = dot_nn(inputs, wv).astype(BF16)
    q_t = dot_nt(wq_t, inputs).astype(BF16)
    k_t = dot_nt(wk_t, inputs).astype(BF16)
    v_t = dot_nt(wv_t, inputs).astype(BF16)
    in_t = dot_nt(eye, inputs).astype(BF16)
    probs, parts = [], []
    for s in groups_of(tokens, members):
        prob = softmax_group(keys[s], q_t[:, s], own)
        probs.append(prob)
        parts.append(attend_group(prob, v_t[:, s], mask))
    att_t = jnp.concatenate(parts, axis=1)
    mixed = dot_nn(dot_nt(back, att_t).astype(BF16), wo).astype(BF16)
    return mixed, (inv, normed, vals, q_t, k_t, in_t, att_t, probs)


def backward_block(gm, saved, wo, there, own, mask):
    inv, normed, vals, q_t, k_t, in_t, att_t, probs = saved
    tokens = gm.shape[0]
    gm = dot_nn(there, gm).astype(BF16)
    ga_t = dot_nt(wo, gm).astype(BF16)
    parts = [
        back_group(prob, vals[s], q_t[:, s], ga_t[:, s], k_t[:, s], own, mask)
        for s, prob in zip(groups_of(tokens, tokens // BLOCK), probs)
    ]
    return (gm,) + tuple(jnp.concatenate(p, axis=1) for p in zip(*parts))


def input_block(gq_t, gk_t, gv_t, saved, gain, wq, wk, wv, back):
    inv, normed = saved[:2]
    rows = [dot_nt(back, g).astype(BF16) for g in (gq_t, gk_t, gv_t)]
    grad_in = dot_nt(rows[0], wq) + dot_nt(rows[1], wk) + dot_nt(rows[2], wv)
    grad_normed = grad_in * gain
    corr = inv * (grad_normed - normed * jnp.mean(grad_normed * normed, axis=-1, keepdims=True))
    return corr.astype(BF16), jnp.sum(grad_in * normed, axis=0, keepdims=True)


def push(src, dst, send_sem, recv_sem, peer):
    return pltpu.make_async_remote_copy(
        src_ref=src, dst_ref=dst, send_sem=send_sem, recv_sem=recv_sem,
        device_id=peer, device_id_type=MESH,
    )


def main_kernel(
    sizes, scale,
    f_hbm, cot_hbm, gain_hbm, wq_hbm, wk_hbm, wv_hbm, wo_hbm, taps_hbm,
    gf_ref, out_ref, small_ref,
    cot, gain_v, wq_v, wk_v, wv_v, wo_v, taps, f_got, gm_src, gm_got, mx_src, mx_got,
    co_src, co_got, row_halo, edges, col_halo, pad,
    g, a_src, a_dst, acc1, b_src, b_dst, c_src, c_dst, ga, s_a, s_b, s_c,
    load, near_send, near_recv, f_send, f_recv, gm_send, gm_recv, mx_send, mx_recv,
    co_send, co_recv, a_send, a_recv, b_send, b_recv, c_send, c_recv, z_send, z_recv,
    p_send, p_recv, g_send, g_recv,
    sa_send, sa_recv, sb_send, sb_recv, sc_send, sc_recv,
):
    count, grid_rows, grid_cols = sizes
    members, rows, cols, width = cot.shape
    cells = f_got.shape[2]
    planes = count // 2 * grid_cols
    unit = g.shape[3]
    mem, row, col = (lax.axis_index(a) for a in ("mem", "row", "col"))
    at = (row, col)
    core, chip = lax.rem(mem, 2), lax.div(mem, 2)
    other = 1 - core
    partner = (mem + 1 - 2 * core, row, col)
    me_p = chip * grid_cols + col

    def plane_peer(p):
        return (lax.div(p, grid_cols) * 2 + core, row, lax.rem(p, grid_cols))

    mem_others = [lax.rem(mem + k, count) for k in range(1, count)]
    plane_others = [lax.rem(me_p + k, planes) for k in range(1, planes)]
    step_z = 1 - 2 * lax.div(row * 2, grid_rows)
    row_others = [
        lax.rem(row + step_z * k + grid_rows, grid_rows) for k in range(1, grid_rows)
    ]

    local = [
        pltpu.make_async_copy(cot_hbm, cot, load.at[0]),
        pltpu.make_async_copy(taps_hbm, taps, load.at[1]),
        pltpu.make_async_copy(wq_hbm, wq_v, load.at[2]),
        pltpu.make_async_copy(wk_hbm, wk_v, load.at[3]),
        pltpu.make_async_copy(wv_hbm, wv_v, load.at[4]),
        pltpu.make_async_copy(wo_hbm, wo_v, load.at[5]),
        pltpu.make_async_copy(gain_hbm, gain_v, load.at[6]),
        pltpu.make_async_copy(f_hbm.at[:, mem], f_got.at[mem], load.at[7]),
    ]
    for copy in local:
        copy.start()

    def exists(step):
        tests = [
            (at[i] > 0) if step[i] < 0 else (at[i] < (grid_rows, grid_cols)[i] - 1)
            for i in range(2)
            if step[i]
        ]
        return functools.reduce(jnp.logical_and, tests)

    def neighbour(step):
        return (mem, row + step[0], col + step[1])

    barrier = pltpu.get_barrier_semaphore()

    def greet(peer):
        pl.semaphore_signal(barrier, inc=1, device_id=peer, device_id_type=MESH)

    greeted = 0
    for r in row_others:
        greet((mem, r, col))
        greeted += 1
    for o in mem_others:
        greet((o, row, col))
        greeted += 1
    for k in range(count // 2):
        for c in range(1, grid_cols):
            there_chip = lax.rem(chip + k, count // 2)
            greet((there_chip * 2 + core, row, lax.rem(col + c, grid_cols)))
            greeted += 1
    diagonal = [step for step in NEAR if step[0] and step[1]]
    for step in diagonal:
        @pl.when(exists(step))
        def _():
            greet(neighbour(step))
    present = sum(exists(step).astype(jnp.int32) for step in diagonal)

    def outgoing(step):
        dr, dc = step
        if dc == 0:
            return cot.at[:, 0 if dr < 0 else rows - 1]
        side = edges.at[0 if dc < 0 else 1]
        return side if dr == 0 else side.at[0 if dr < 0 else rows - 1]

    def landing(step):
        dr, dc = step
        if dc == 0:
            return row_halo.at[0 if dr < 0 else 1]
        side = col_halo.at[0 if dc < 0 else 1]
        return side.at[pl.ds(1, rows)] if dr == 0 else side.at[0 if dr < 0 else rows + 1]

    def halo_copy(i):
        step = NEAR[i]
        back_i = len(NEAR) - 1 - i
        return push(
            outgoing(step), landing(NEAR[back_i]), near_send.at[i], near_recv.at[back_i],
            neighbour(step),
        )

    local[0].wait()
    pad[:, 1 : rows + 1, EDGE : EDGE + cols, :] = cot[...].astype(F32)
    for m in range(members):
        for r in range(rows):
            edges[0, r, m : m + 1] = cot[m, r, 0:BLOCK].astype(F32)[:1]
            edges[1, r, m : m + 1] = cot[m, r, cols - BLOCK : cols].astype(F32)[BLOCK - 1 :]
    for i in range(len(NEAR)):
        @pl.when(jnp.logical_not(exists(NEAR[i])))
        def _():
            there_ref = landing(NEAR[i])
            there_ref[...] = jnp.zeros(there_ref.shape, there_ref.dtype)

    pl.semaphore_wait(barrier, present + greeted)

    for i in range(len(NEAR)):
        @pl.when(exists(NEAR[i]))
        def _():
            halo_copy(i).start()
    sent = []

    def start(copy):
        copy.start()
        sent.append(copy)

    for o in mem_others:
        start(push(f_hbm.at[:, o], f_got.at[mem], f_send.at[o], f_recv.at[mem], (o, *at)))

    for copy in local[1:]:
        copy.wait()
    eye = one_hot(width, lambda i: i)
    there, back = cell_first(count * members)
    own, mask = cell_masks(count * members)
    wq, wk, wv, wo = (w[...] for w in (wq_v, wk_v, wv_v, wo_v))
    wq_t, wk_t, wv_t = (dot_nt(eye, w).astype(BF16) for w in (wq, wk, wv))
    gain = gain_v[...]
    taps9 = [[taps[i, j : j + 1, :] for j in range(3)] for i in range(3)]

    for i in range(len(NEAR)):
        @pl.when(exists(NEAR[i]))
        def _():
            there_ref = landing(NEAR[i])
            push(
                there_ref, there_ref, near_send.at[i], near_recv.at[i], neighbour(NEAR[i])
            ).wait_recv()
    pad[:, 0, EDGE : EDGE + cols, :] = row_halo[0].astype(F32)
    pad[:, rows + 1, EDGE : EDGE + cols, :] = row_halo[1].astype(F32)
    for side, place in ((0, EDGE - 1), (1, EDGE + cols)):
        for r in range(rows + 2):
            column = col_halo[side, r]
            for m in range(members):
                pad[m, r, place : place + 1, :] = column[m : m + 1]

    seg = min(cells, cols)

    def segments(j):
        for s in range(cells // seg):
            cell = j * cells + s * seg
            yield s * seg, cell // cols, cell % cols

    for j in range(count):
        for first, r, c in segments(j):
            for m in range(members):
                wins = [pad[m, 2 - i + r, c : c + seg + 2 * EDGE, :] for i in range(3)]
                cols3 = [sum(taps9[i][k] * wins[i] for i in range(3)) for k in range(3)]
                summed = sum(
                    cols3[k][EDGE + 1 - k : EDGE + 1 - k + seg] for k in range(3)
                )
                gm_src[m, j, first : first + seg, :] = summed.astype(BF16)

        @pl.when(mem != j)
        def _():
            push(gm_src.at[:, j], gm_got.at[mem], gm_send.at[j], gm_recv.at[mem], (j, *at)).start()

        @pl.when(mem == j)
        def _():
            gm_got[j] = gm_src[:, j]

    for o in mem_others:
        push(f_hbm.at[:, o], f_got.at[o], f_send.at[o], f_recv.at[o], (o, *at)).wait_recv()
    blocks = [slice(i, i + BLOCK) for i in range(0, cells, BLOCK)]
    tokens = count * members * BLOCK
    saved = []
    for b in blocks:
        x = f_got[:, :, b, :].reshape(tokens, width).astype(F32)
        mixed, keep = forward_block(
            x, gain, wq_t, wk_t, wv_t, wk, wv, wo, there, back, eye, own, mask
        )
        mx_src[:, :, b, :] = mixed.reshape(count, members, BLOCK, width)
        saved.append(keep)
    for o in mem_others:
        start(push(mx_src.at[o], mx_got.at[:, mem], mx_send.at[o], mx_recv.at[mem], (o, *at)))
    mx_got[:, mem] = mx_src[mem]

    for o in mem_others:
        push(gm_src.at[:, o], gm_got.at[o], gm_send.at[o], gm_recv.at[o], (o, *at)).wait_recv()
    grads = [
        backward_block(gm_got[:, :, b, :].reshape(tokens, width), keep, wo, there, own, mask)
        for b, keep in zip(blocks, saved)
    ]
    gms = jnp.concatenate([x[0] for x in grads], axis=0)
    in_t = jnp.concatenate([keep[5] for keep in saved], axis=1)
    att_t = jnp.concatenate([keep[6] for keep in saved], axis=1)
    wholes = [
        dot_nt(in_t, jnp.concatenate([x[i] for x in grads], axis=1)) for i in (1, 2, 3)
    ] + [dot_nn(att_t, gms)]
    for i, value in enumerate(wholes):
        for k in range(width // unit):
            flat = i * (width // unit) + k
            half, rest = divmod(flat, planes * grid_rows)
            g[half, rest // grid_rows, rest % grid_rows] = value[k * unit : (k + 1) * unit]

    a_src[...] = g[other].astype(BF16)
    first_copy = push(a_src, a_dst, a_send, a_recv, partner)
    first_copy.start()
    gain_sum = jnp.zeros((1, width), F32)
    for b, keep, x in zip(blocks, saved, grads):
        corr, part = input_block(*x[1:], keep, gain, wq, wk, wv, back)
        co_src[:, :, b, :] = corr.reshape(count, members, BLOCK, width)
        gain_sum = gain_sum + part
    first_copy.wait()
    acc1[...] = g[core] + a_dst[...].astype(F32)
    b_src[...] = acc1[...].astype(BF16)
    turns = row_others[::-1] + [row]
    for r in turns:
        for p in plane_others:
            start(push(
                b_src.at[p, r], b_dst.at[me_p, r], b_send.at[p, r], b_recv.at[me_p, r],
                plane_peer(p),
            ))
    for o in mem_others:
        start(push(co_src.at[o], co_got.at[:, mem], co_send.at[o], co_recv.at[mem], (o, *at)))
    co_got[:, mem] = co_src[mem]

    for o in mem_others:
        push(mx_src.at[o], mx_got.at[:, o], mx_send.at[o], mx_recv.at[o], (o, *at)).wait_recv()
    kernel_sum = [[jnp.zeros((8, width), F32) for _ in range(3)] for _ in range(3)]
    for j in range(count):
        for first, r, c in segments(j):
            for m in range(members):
                mx = mx_got[m, j, first : first + seg, :].astype(F32)
                for k in range(3):
                    ahead = EDGE + 1 - k
                    wide = jnp.concatenate(
                        [
                            jnp.zeros((ahead, width), F32), mx,
                            jnp.zeros((2 * EDGE - ahead, width), F32),
                        ],
                        axis=0,
                    )
                    for i in range(3):
                        win = pad[m, 2 - i + r, c : c + seg + 2 * EDGE, :]
                        product = (wide * win).reshape(-1, 8, width)
                        kernel_sum[i][k] = kernel_sum[i][k] + jnp.sum(product, axis=0)
    s_a[core] = jnp.concatenate(
        [gain_sum]
        + [jnp.sum(kernel_sum[i][k], axis=0, keepdims=True) for i in range(3) for k in range(3)]
        + [jnp.zeros((6, width), F32)],
        axis=0,
    )
    start(push(s_a.at[core], s_a.at[core], sa_send, sa_recv, partner))

    for r in turns:
        for p in plane_others:
            push(
                b_src.at[p, r], b_dst.at[p, r], b_send.at[p, r], b_recv.at[p, r], plane_peer(p)
            ).wait_recv()
        whole = acc1[me_p, r]
        for p in plane_others:
            whole = whole + b_dst[p, r].astype(F32)
        if r is not row:
            c_src[r] = whole.astype(BF16)
            start(push(c_src.at[r], c_dst.at[row], c_send.at[r], c_recv.at[row], (mem, r, col)))
    push(s_a.at[other], s_a.at[other], sa_send, sa_recv, partner).wait_recv()
    s_b[me_p] = s_a[0] + s_a[1]
    for p in plane_others:
        start(push(
            s_b.at[me_p], s_b.at[me_p], sb_send.at[p], sb_recv.at[me_p], plane_peer(p)
        ))
    for r in row_others:
        push(c_src.at[r], c_dst.at[r], c_send.at[r], c_recv.at[r], (mem, r, col)).wait_recv()
        whole = whole + c_dst[r].astype(F32)
    ga[core, me_p, row] = (whole * scale).astype(BF16)

    for r in row_others:
        piece = ga.at[core, me_p, row]
        start(push(piece, piece, z_send.at[r], z_recv.at[row], (mem, r, col)))

    def to_partner(p, r):
        piece = ga.at[core, p, r]
        start(push(piece, piece, g_send.at[p, r], g_recv.at[p, r], partner))
        out_ref[core, p, r] = ga[core, p, r].astype(F32)

    def to_plane(r):
        piece = ga.at[core, me_p, r]
        for p in plane_others:
            start(push(piece, piece, p_send.at[p, r], p_recv.at[me_p, r], plane_peer(p)))
        to_partner(me_p, r)

    def from_plane(r):
        for p in plane_others:
            piece = ga.at[core, p, r]
            push(piece, piece, p_send.at[p, r], p_recv.at[p, r], plane_peer(p)).wait_recv()
            to_partner(p, r)

    to_plane(row)
    for p in plane_others:
        push(s_b.at[p], s_b.at[p], sb_send.at[p], sb_recv.at[p], plane_peer(p)).wait_recv()
    s_c[row] = sum(s_b[p] for p in range(planes))
    for r in row_others:
        start(push(s_c.at[row], s_c.at[row], sc_send.at[r], sc_recv.at[row], (mem, r, col)))
    for o in mem_others:
        push(co_src.at[o], co_got.at[:, o], co_send.at[o], co_recv.at[o], (o, *at)).wait_recv()
    gf_ref[...] = (
        cot[...].astype(F32) + co_got[...].reshape(cot.shape).astype(F32)
    ).astype(BF16)

    before = row
    for r in row_others:
        piece = ga.at[core, me_p, r]
        push(piece, piece, z_send.at[r], z_recv.at[r], (mem, r, col)).wait_recv()
        to_plane(r)
        from_plane(before)
        before = r
    from_plane(before)
    for r in row_others:
        push(s_c.at[r], s_c.at[r], sc_send.at[r], sc_recv.at[r], (mem, r, col)).wait_recv()
    small_ref[...] = sum(s_c[r] for r in range(grid_rows)) * scale
    for r in [row] + row_others:
        for p in [me_p] + plane_others:
            piece = ga.at[other, p, r]
            push(piece, piece, g_send.at[p, r], g_recv.at[p, r], partner).wait_recv()
            out_ref[other, p, r] = ga[other, p, r].astype(F32)

    for copy in sent:
        copy.wait_send()
    for i in range(len(NEAR)):
        @pl.when(exists(NEAR[i]))
        def _():
            halo_copy(i).wait_send()
    for j in range(count):
        @pl.when(mem != j)
        def _():
            push(
                gm_src.at[:, j], gm_got.at[mem], gm_send.at[j], gm_recv.at[mem], (j, *at)
            ).wait_send()


def output_kernel(
    gf_in, out_in, small_in, gf, gain, gq, gk, gv, go, taps, taps_v, sems,
):
    copies = [
        pltpu.make_async_copy(out_in.at[i], ref, sems.at[i]) for i, ref in enumerate((gq, gk, gv, go))
    ]
    copies.append(pltpu.make_async_copy(gf_in, gf, sems.at[4]))
    copies.append(pltpu.make_async_copy(small_in.at[pl.ds(0, 1)], gain, sems.at[5]))
    for copy in copies:
        copy.start()
    for i in range(3):
        taps_v[i] = small_in[1 + 3 * i : 4 + 3 * i, :]
    last = pltpu.make_async_copy(taps_v, taps, sems.at[6])
    last.start()
    for copy in copies:
        copy.wait()
    last.wait()


def local(fields, norm_gain, w_query, w_key, w_value, w_out, mix_kernel, cotangent):
    members, rows, cols, width = fields.shape
    count, grid_rows, grid_cols = (lax.axis_size(a) for a in ("mem", "row", "col"))
    cells = rows * cols // count
    planes = count // 2 * grid_cols
    height = 4 * width
    unit = height // (2 * planes * grid_rows)
    tokens = math.prod(fields.shape[:3]) * count * grid_rows * grid_cols
    sems = pltpu.SemaphoreType.DMA
    vmem = pltpu.VMEM
    split = (members, count, cells, width)
    got = (count, members, cells, width)
    square = vmem((width, width), BF16)
    half = (planes, grid_rows, unit, width)
    line = (grid_rows, unit, width)
    small = (16, width)

    def pair(shape):
        return [sems(shape), sems(shape)]

    gf, out, small_sum = pl.pallas_call(
        functools.partial(
            main_kernel, (count, grid_rows, grid_cols), 1.0 / math.sqrt(tokens)
        ),
        out_shape=(
            jax.ShapeDtypeStruct(fields.shape, BF16),
            jax.ShapeDtypeStruct((2,) + half, F32),
            jax.ShapeDtypeStruct(small, F32),
        ),
        in_specs=[HBM_SPEC] * 8,
        out_specs=(VMEM_SPEC,) * 3,
        scratch_shapes=[
            vmem(fields.shape, BF16), vmem((1, width), F32), square, square, square, square,
            vmem((3, 3, width), F32),
            vmem(got, BF16), vmem(split, BF16), vmem(got, BF16), vmem(got, BF16), vmem(split, BF16),
            vmem(got, BF16), vmem(split, BF16),
            vmem((2, members, cols, width), BF16),
            vmem((2, rows, members, width), F32), vmem((2, rows + 2, members, width), F32),
            vmem((members, rows + 2, cols + 2 * EDGE, width), F32),
            vmem((2,) + half, F32), vmem(half, BF16), vmem(half, BF16), vmem(half, F32),
            vmem(half, BF16), vmem(half, BF16), vmem(line, BF16), vmem(line, BF16),
            vmem((2,) + half, BF16),
            vmem((2,) + small, F32), vmem((planes,) + small, F32), vmem((grid_rows,) + small, F32),
            sems((8,)), *pair((len(NEAR),)),
            *pair((count,)), *pair((count,)), *pair((count,)), *pair((count,)),
            *pair(()), *pair((planes, grid_rows)), *pair((grid_rows,)), *pair((grid_rows,)),
            *pair((planes, grid_rows)), *pair((planes, grid_rows)),
            *pair(()), *pair((planes,)), *pair((grid_rows,)),
        ],
        compiler_params=pltpu.CompilerParams(
            collective_id=1, has_side_effects=True, vmem_limit_bytes=24 * 2**20
        ),
    )(*(
        pltpu.with_memory_space_constraint(x, pltpu.HBM)
        for x in (
            fields.reshape(split), cotangent, norm_gain.reshape(1, -1),
            w_query, w_key, w_value, w_out, mix_kernel,
        )
    ))
    square32 = jax.ShapeDtypeStruct((width, width), F32)
    gf, gain, gq, gk, gv, go, taps = pl.pallas_call(
        output_kernel,
        out_shape=(
            jax.ShapeDtypeStruct(fields.shape, BF16), jax.ShapeDtypeStruct((1, width), F32),
            square32, square32, square32, square32,
            jax.ShapeDtypeStruct((3, 3, width), F32),
        ),
        in_specs=[VMEM_SPEC] * 3,
        out_specs=(HBM_SPEC,) * 7,
        scratch_shapes=[vmem((3, 3, width), F32), sems((7,))],
        compiler_params=pltpu.CompilerParams(vmem_limit_bytes=16 * 2**20),
    )(gf, out.reshape(4, width, width), small_sum)
    return (gf, gain.reshape(-1), gq, gk, gv, go, taps)


def solution(mesh):
    tile = P("mem", "row", "col", None)
    in_specs = (tile, P(), P(), P(), P(), P(), P(), tile)
    out_specs = (tile, P(), P(), P(), P(), P(), P())
    return jax.shard_map(local, mesh=mesh, in_specs=in_specs, out_specs=out_specs, check_vma=False)
```

```python
import functools
import math

import jax
import jax.numpy as jnp
from jax import lax
from jax.experimental import pallas as pl
from jax.experimental.pallas import tpu as pltpu
from jax.sharding import PartitionSpec as P

HEADS = 8
SUB = 8
BLOCK = 16
EDGE = 8

epsilon = 1e-06
F32 = jnp.float32
BF16 = jnp.bfloat16
MESH = pl.DeviceIdType.MESH
VMEM_SPEC = pl.BlockSpec(memory_space=pltpu.VMEM)
HBM_SPEC = pl.BlockSpec(memory_space=pltpu.HBM)
NEAR = [(dr, dc) for dr in (-1, 0, 1) for dc in (-1, 0, 1) if (dr, dc) != (0, 0)]


def dot_nn(a, b):
    return lax.dot_general(a, b, (((1,), (0,)), ((), ())), preferred_element_type=F32)


def dot_nt(a, b):
    return lax.dot_general(a, b, (((1,), (1,)), ((), ())), preferred_element_type=F32)


def one_hot(size, target):
    row = lax.broadcasted_iota(jnp.int32, (size, size), 0)
    col = lax.broadcasted_iota(jnp.int32, (size, size), 1)
    return jnp.where(target(row) == col, 1.0, 0.0).astype(BF16)


def cell_first(members):
    size = members * BLOCK
    there = one_hot(size, lambda i: lax.rem(i, members) * BLOCK + lax.div(i, members))
    back = one_hot(size, lambda i: lax.rem(i, BLOCK) * members + lax.div(i, BLOCK))
    return there, back


def cell_masks(members):
    tokens = SUB * members
    lane = lax.div(lax.broadcasted_iota(jnp.int32, (members, tokens), 1), members)
    own = [lane == c for c in range(SUB)]
    return own, [jnp.where(o, 1.0, 0.0).astype(BF16) for o in own]


def own_cells(left, right_t, own):
    tokens, width = left.shape
    members = tokens // SUB
    dim = width // HEADS
    zeros = jnp.zeros((dim, tokens), right_t.dtype)
    heads = []
    for h in range(0, HEADS, 2):
        pair = [
            jnp.concatenate(
                [right_t[k * dim : (k + 1) * dim] if k == p else zeros for k in range(HEADS)], axis=0
            )
            for p in (h, h + 1)
        ]
        both = dot_nn(left, jnp.concatenate(pair, axis=1))
        for i in range(2):
            full = both[:, i * tokens : (i + 1) * tokens]
            picked = full[:members]
            for c in range(1, SUB):
                picked = jnp.where(own[c], full[c * members : (c + 1) * members], picked)
            heads.append(picked)
    return jnp.stack(heads)


def spread(packed, mask):
    return jnp.concatenate([packed * m for m in mask], axis=0)


def softmax_group(keys, q_t, own):
    dim = keys.shape[1] // HEADS
    scores = own_cells(keys, q_t, own) * (1.0 / math.sqrt(dim))
    lifted = jnp.exp(scores - jnp.max(scores, axis=1, keepdims=True))
    return lifted * (1.0 / jnp.sum(lifted, axis=1, keepdims=True))


def attend_group(prob, v_t, mask):
    dim = v_t.shape[0] // HEADS
    return jnp.concatenate(
        [
            dot_nn(v_t[h * dim : (h + 1) * dim], spread(prob[h].astype(BF16), mask))
            for h in range(HEADS)
        ],
        axis=0,
    ).astype(BF16)


def back_values(prob, ga_t, mask):
    dim = ga_t.shape[0] // HEADS
    return jnp.concatenate(
        [
            dot_nt(ga_t[h * dim : (h + 1) * dim], spread(prob[h].astype(BF16), mask))
            for h in range(HEADS)
        ],
        axis=0,
    ).astype(BF16)


def back_scores(prob, vals, q_t, ga_t, k_t, own, mask):
    dim = vals.shape[1] // HEADS
    grad_prob = own_cells(vals, ga_t, own)
    inner = jnp.sum(prob * grad_prob, axis=1, keepdims=True)
    grad_score = prob * (grad_prob - inner) * (1.0 / math.sqrt(dim))
    outs = ([], [])
    for h in range(HEADS):
        hs = slice(h * dim, (h + 1) * dim)
        gs = spread(grad_score[h].astype(BF16), mask)
        outs[0].append(dot_nn(k_t[hs], gs))
        outs[1].append(dot_nt(q_t[hs], gs))
    return tuple(jnp.concatenate(o, axis=0).astype(BF16) for o in outs)


def groups_of(tokens, members):
    size = SUB * members
    return [slice(i, i + size) for i in range(0, tokens, size)]


def forward_block(x, gain, wq_t, wk_t, wv_t, wk, wv, wo, there, back, eye, own, mask):
    tokens = x.shape[0]
    members = tokens // BLOCK
    inv = lax.rsqrt(jnp.mean(x * x, axis=-1, keepdims=True) + epsilon)
    normed = x * inv
    inputs = dot_nn(there, (normed * gain).astype(BF16)).astype(BF16)
    keys = dot_nn(inputs, wk).astype(BF16)
    vals = dot_nn(inputs, wv).astype(BF16)
    q_t = dot_nt(wq_t, inputs).astype(BF16)
    k_t = dot_nt(wk_t, inputs).astype(BF16)
    v_t = dot_nt(wv_t, inputs).astype(BF16)
    in_t = dot_nt(eye, inputs).astype(BF16)
    probs, parts = [], []
    for s in groups_of(tokens, members):
        prob = softmax_group(keys[s], q_t[:, s], own)
        probs.append(prob)
        parts.append(attend_group(prob, v_t[:, s], mask))
    att_t = jnp.concatenate(parts, axis=1)
    mixed = dot_nn(dot_nt(back, att_t).astype(BF16), wo).astype(BF16)
    return mixed, (inv, normed, vals, q_t, k_t, in_t, att_t, probs)


def early_block(gm, saved, wo, there, mask):
    probs = saved[-1]
    gm = dot_nn(there, gm).astype(BF16)
    ga_t = dot_nt(wo, gm).astype(BF16)
    cuts = groups_of(gm.shape[0], gm.shape[0] // BLOCK)
    gv_t = jnp.concatenate(
        [back_values(prob, ga_t[:, s], mask) for s, prob in zip(cuts, probs)], axis=1
    )
    return gm, ga_t, gv_t


def late_block(ga_t, saved, own, mask):
    inv, normed, vals, q_t, k_t, in_t, att_t, probs = saved
    tokens = vals.shape[0]
    parts = [
        back_scores(prob, vals[s], q_t[:, s], ga_t[:, s], k_t[:, s], own, mask)
        for s, prob in zip(groups_of(tokens, tokens // BLOCK), probs)
    ]
    return tuple(jnp.concatenate(p, axis=1) for p in zip(*parts))


def input_block(gq_t, gk_t, gv_t, saved, gain, wq, wk, wv, back):
    inv, normed = saved[:2]
    rows = [dot_nt(back, g).astype(BF16) for g in (gq_t, gk_t, gv_t)]
    grad_in = dot_nt(rows[0], wq) + dot_nt(rows[1], wk) + dot_nt(rows[2], wv)
    grad_normed = grad_in * gain
    corr = inv * (grad_normed - normed * jnp.mean(grad_normed * normed, axis=-1, keepdims=True))
    return corr.astype(BF16), jnp.sum(grad_in * normed, axis=0, keepdims=True)


def push(src, dst, send_sem, recv_sem, peer):
    return pltpu.make_async_remote_copy(
        src_ref=src, dst_ref=dst, send_sem=send_sem, recv_sem=recv_sem,
        device_id=peer, device_id_type=MESH,
    )


def main_kernel(
    sizes, scale,
    f_hbm, cot_hbm, gain_hbm, wq_hbm, wk_hbm, wv_hbm, wo_hbm, taps_hbm,
    gf_ref, out_ref, small_ref,
    cot, gain_v, wq_v, wk_v, wv_v, wo_v, taps, f_got, gm_src, gm_got, mx_src, mx_got,
    co_src, co_got, row_halo, edges, col_halo, pad,
    g, a_src, a_dst, acc, b_src, b_dst, c_all, ga, s_a, s_b, s_c,
    load, near_send, near_recv, f_send, f_recv, gm_send, gm_recv, mx_send, mx_recv,
    co_send, co_recv, a_send, a_recv, b_send, b_recv, c_send, c_recv,
    p_send, p_recv, g_send, g_recv,
    sa_send, sa_recv, sb_send, sb_recv, sc_send, sc_recv,
):
    count, grid_rows, grid_cols = sizes
    members, rows, cols, width = cot.shape
    cells = f_got.shape[2]
    planes = count // 2 * grid_cols
    subs, unit = g.shape[3:5]
    mem, row, col = (lax.axis_index(a) for a in ("mem", "row", "col"))
    at = (row, col)
    core, chip = lax.rem(mem, 2), lax.div(mem, 2)
    other = 1 - core
    partner = (mem + 1 - 2 * core, row, col)
    me_p = chip * grid_cols + col

    def plane_peer(p):
        return (lax.div(p, grid_cols) * 2 + core, row, lax.rem(p, grid_cols))

    mem_others = [
        lax.rem(chip + k, count // 2) * 2 + c for k in range(1, count // 2) for c in (core, other)
    ] + [partner[0]]
    plane_others = [lax.rem(me_p + k, planes) for k in range(1, planes)]
    step_z = 1 - 2 * lax.div(row * 2, grid_rows)
    row_others = [
        lax.rem(row + step_z * k + grid_rows, grid_rows) for k in range(1, grid_rows)
    ]

    far_rows = row_others[::-1]
    local = [
        pltpu.make_async_copy(cot_hbm, cot, load.at[0]),
        pltpu.make_async_copy(taps_hbm, taps, load.at[1]),
        pltpu.make_async_copy(wq_hbm, wq_v, load.at[2]),
        pltpu.make_async_copy(wk_hbm, wk_v, load.at[3]),
        pltpu.make_async_copy(wv_hbm, wv_v, load.at[4]),
        pltpu.make_async_copy(wo_hbm, wo_v, load.at[5]),
        pltpu.make_async_copy(gain_hbm, gain_v, load.at[6]),
        pltpu.make_async_copy(f_hbm.at[:, mem], f_got.at[mem], load.at[7]),
    ]
    for copy in local:
        copy.start()

    def exists(step):
        tests = [
            (at[i] > 0) if step[i] < 0 else (at[i] < (grid_rows, grid_cols)[i] - 1)
            for i in range(2)
            if step[i]
        ]
        return functools.reduce(jnp.logical_and, tests)

    def neighbour(step):
        return (mem, row + step[0], col + step[1])

    barrier = pltpu.get_barrier_semaphore()

    def greet(peer):
        pl.semaphore_signal(barrier, inc=1, device_id=peer, device_id_type=MESH)

    greeted = 0
    for r in row_others:
        greet((mem, r, col))
        greeted += 1
    for o in mem_others:
        greet((o, row, col))
        greeted += 1
    for k in range(count // 2):
        for c in range(1, grid_cols):
            there_chip = lax.rem(chip + k, count // 2)
            greet((there_chip * 2 + core, row, lax.rem(col + c, grid_cols)))
            greeted += 1
    diagonal = [step for step in NEAR if step[0] and step[1]]
    for step in diagonal:
        @pl.when(exists(step))
        def _():
            greet(neighbour(step))
    present = sum(exists(step).astype(jnp.int32) for step in diagonal)

    def outgoing(step):
        dr, dc = step
        if dc == 0:
            return cot.at[:, 0 if dr < 0 else rows - 1]
        side = edges.at[0 if dc < 0 else 1]
        return side if dr == 0 else side.at[0 if dr < 0 else rows - 1]

    def landing(step):
        dr, dc = step
        if dc == 0:
            return row_halo.at[0 if dr < 0 else 1]
        side = col_halo.at[0 if dc < 0 else 1]
        return side.at[pl.ds(1, rows)] if dr == 0 else side.at[0 if dr < 0 else rows + 1]

    def halo_copy(i):
        step = NEAR[i]
        back_i = len(NEAR) - 1 - i
        return push(
            outgoing(step), landing(NEAR[back_i]), near_send.at[i], near_recv.at[back_i],
            neighbour(step),
        )

    straight = [i for i in range(len(NEAR)) if NEAR[i][1] == 0]
    sideways = [i for i in range(len(NEAR)) if NEAR[i][1] != 0]
    sent = []

    def start(copy):
        copy.start()
        sent.append(copy)

    def send_halo(steps):
        for i in steps:
            @pl.when(exists(NEAR[i]))
            def _():
                halo_copy(i).start()

    def wait_halo(steps):
        for i in steps:
            @pl.when(exists(NEAR[i]))
            def _():
                there_ref = landing(NEAR[i])
                push(
                    there_ref, there_ref, near_send.at[i], near_recv.at[i], neighbour(NEAR[i])
                ).wait_recv()

    for i in range(len(NEAR)):
        @pl.when(jnp.logical_not(exists(NEAR[i])))
        def _():
            there_ref = landing(NEAR[i])
            there_ref[...] = jnp.zeros(there_ref.shape, there_ref.dtype)
    blocks = [slice(i, i + BLOCK) for i in range(0, cells, BLOCK)]

    local[0].wait()
    pad[:, 1 : rows + 1, EDGE : EDGE + cols, :] = cot[...].astype(F32)
    for m in range(members):
        for r in range(rows):
            edges[0, r, m : m + 1] = cot[m, r, 0:BLOCK].astype(F32)[:1]
            edges[1, r, m : m + 1] = cot[m, r, cols - BLOCK : cols].astype(F32)[BLOCK - 1 :]
    pl.semaphore_wait(barrier, present + greeted)
    send_halo(sideways)
    send_halo(straight)
    for i, b in enumerate(blocks):
        for o in mem_others:
            start(push(
                f_hbm.at[:, o, b], f_got.at[mem, :, b], f_send.at[o, i], f_recv.at[mem, i], (o, *at)
            ))
    for copy in local[1:]:
        copy.wait()
    eye = one_hot(width, lambda i: i)
    there, back = cell_first(count * members)
    own, mask = cell_masks(count * members)
    wq, wk, wv, wo = (w[...] for w in (wq_v, wk_v, wv_v, wo_v))
    wq_t, wk_t, wv_t = (dot_nt(eye, w).astype(BF16) for w in (wq, wk, wv))
    gain = gain_v[...]
    taps9 = [[taps[i, j : j + 1, :] for j in range(3)] for i in range(3)]

    wait_halo(sideways)
    for side, place in ((0, EDGE - 1), (1, EDGE + cols)):
        for r in range(rows + 2):
            column = col_halo[side, r]
            for m in range(members):
                pad[m, r, place : place + 1, :] = column[m : m + 1]

    seg = min(cells, cols)

    def segments(j):
        for s in range(cells // seg):
            cell = j * cells + s * seg
            yield s * seg, cell // cols, cell % cols

    def send_mixed_gradient(j):
        for first, r, c in segments(j):
            for m in range(members):
                wins = [pad[m, 2 - i + r, c : c + seg + 2 * EDGE, :] for i in range(3)]
                cols3 = [sum(taps9[i][k] * wins[i] for i in range(3)) for k in range(3)]
                summed = sum(
                    cols3[k][EDGE + 1 - k : EDGE + 1 - k + seg] for k in range(3)
                )
                gm_src[m, j, first : first + seg, :] = summed.astype(BF16)

        @pl.when(mem != j)
        def _():
            push(gm_src.at[:, j], gm_got.at[mem], gm_send.at[j], gm_recv.at[mem], (j, *at)).start()

        @pl.when(mem == j)
        def _():
            gm_got[j] = gm_src[:, j]

    def inner(j):
        return all(0 < r < rows - 1 for _, r, _ in segments(j))

    for j in range(count):
        if inner(j):
            send_mixed_gradient(j)
    wait_halo(straight)
    pad[:, 0, EDGE : EDGE + cols, :] = row_halo[0].astype(F32)
    pad[:, rows + 1, EDGE : EDGE + cols, :] = row_halo[1].astype(F32)
    for j in range(count):
        if not inner(j):
            send_mixed_gradient(j)

    tokens = count * members * BLOCK
    saved = []
    for i, b in enumerate(blocks):
        for o in mem_others:
            push(
                f_hbm.at[:, o, b], f_got.at[o, :, b], f_send.at[o, i], f_recv.at[o, i], (o, *at)
            ).wait_recv()
        x = f_got[:, :, b, :].reshape(tokens, width).astype(F32)
        mixed, keep = forward_block(
            x, gain, wq_t, wk_t, wv_t, wk, wv, wo, there, back, eye, own, mask
        )
        mx_src[:, :, b, :] = mixed.reshape(count, members, BLOCK, width)
        saved.append(keep)
    for i, b in enumerate(blocks):
        for o in mem_others:
            start(push(
                mx_src.at[o, :, b], mx_got.at[:, mem, b], mx_send.at[o, i], mx_recv.at[mem, i],
                (o, *at),
            ))
    mx_got[:, mem] = mx_src[mem]

    for o in mem_others:
        push(gm_src.at[:, o], gm_got.at[o], gm_send.at[o], gm_recv.at[o], (o, *at)).wait_recv()
    def store(chunk, values):
        for half, value in enumerate(values):
            for k in range(width // unit):
                g[chunk, half, k // subs, k % subs] = value[k * unit : (k + 1) * unit]

    def to_core(chunk):
        a_src[chunk] = g[chunk, other].astype(BF16)
        start(push(
            a_src.at[chunk], a_dst.at[chunk], a_send.at[chunk], a_recv.at[chunk], partner
        ))

    def to_owner(chunk):
        push(
            a_src.at[chunk], a_dst.at[chunk], a_send.at[chunk], a_recv.at[chunk], partner
        ).wait_recv()
        acc[chunk] = g[chunk, core] + a_dst[chunk].astype(F32)
        b_src[chunk] = acc[chunk].astype(BF16)
        for s in range(subs):
            for p in plane_others:
                start(push(
                    b_src.at[chunk, p, s], b_dst.at[chunk, me_p, s],
                    b_send.at[chunk, p, s], b_recv.at[chunk, me_p, s], plane_peer(p),
                ))

    def to_rows(chunk):
        for s in range(subs):
            for p in plane_others:
                push(
                    b_src.at[chunk, p, s], b_dst.at[chunk, p, s],
                    b_send.at[chunk, p, s], b_recv.at[chunk, p, s], plane_peer(p),
                ).wait_recv()
            whole = acc[chunk, me_p, s]
            for p in plane_others:
                whole = whole + b_dst[chunk, p, s].astype(F32)
            c_all[chunk, s, row] = whole.astype(BF16)
            for r in far_rows:
                piece = c_all.at[chunk, s, row]
                start(push(
                    piece, piece, c_send.at[chunk, s, r], c_recv.at[chunk, s, row], (mem, r, col)
                ))

    def to_partner(chunk, p, s):
        piece = ga.at[chunk, core, p, s]
        start(push(
            piece, piece, g_send.at[chunk, p, s], g_recv.at[chunk, p, s], partner
        ))
        out_ref[chunk, core, p, s] = ga[chunk, core, p, s].astype(F32)

    def to_plane(chunk):
        for s in range(subs):
            for r in row_others:
                piece = c_all.at[chunk, s, r]
                push(
                    piece, piece, c_send.at[chunk, s, r], c_recv.at[chunk, s, r], (mem, r, col)
                ).wait_recv()
            whole = sum(c_all[chunk, s, r].astype(F32) for r in range(grid_rows))
            ga[chunk, core, me_p, s] = (whole * scale).astype(BF16)
            piece = ga.at[chunk, core, me_p, s]
            for p in plane_others:
                start(push(
                    piece, piece, p_send.at[chunk, p, s], p_recv.at[chunk, me_p, s], plane_peer(p)
                ))
            to_partner(chunk, me_p, s)

    def from_plane(chunk):
        for s in range(subs):
            for p in plane_others:
                piece = ga.at[chunk, core, p, s]
                push(
                    piece, piece, p_send.at[chunk, p, s], p_recv.at[chunk, p, s], plane_peer(p)
                ).wait_recv()
                to_partner(chunk, p, s)

    def from_partner(chunk):
        for s in range(subs):
            for p in [me_p] + plane_others:
                piece = ga.at[chunk, other, p, s]
                push(
                    piece, piece, g_send.at[chunk, p, s], g_recv.at[chunk, p, s], partner
                ).wait_recv()
                out_ref[chunk, other, p, s] = ga[chunk, other, p, s].astype(F32)

    early = [
        early_block(gm_got[:, :, b, :].reshape(tokens, width), keep, wo, there, mask)
        for b, keep in zip(blocks, saved)
    ]
    in_t = jnp.concatenate([keep[5] for keep in saved], axis=1)
    att_t = jnp.concatenate([keep[6] for keep in saved], axis=1)
    store(0, (
        dot_nt(in_t, jnp.concatenate([x[2] for x in early], axis=1)),
        dot_nn(att_t, jnp.concatenate([x[0] for x in early], axis=0)),
    ))
    to_core(0)
    late = []
    for i, (x, keep) in enumerate(zip(early, saved)):
        late.append(late_block(x[1], keep, own, mask))
        if i == 0:
            to_owner(0)
    store(1, tuple(
        dot_nt(in_t, jnp.concatenate([x[i] for x in late], axis=1)) for i in range(2)
    ))
    to_core(1)
    gain_sum = jnp.zeros((1, width), F32)
    for b, keep, x, y in zip(blocks, saved, early, late):
        corr, part = input_block(*y, x[2], keep, gain, wq, wk, wv, back)
        co_src[:, :, b, :] = corr.reshape(count, members, BLOCK, width)
        gain_sum = gain_sum + part
    to_owner(1)
    for o in mem_others:
        start(push(co_src.at[o], co_got.at[:, mem], co_send.at[o], co_recv.at[mem], (o, *at)))
    co_got[:, mem] = co_src[mem]
    for i, b in enumerate(blocks):
        for o in mem_others:
            push(
                mx_src.at[o, :, b], mx_got.at[:, o, b], mx_send.at[o, i], mx_recv.at[o, i],
                (o, *at),
            ).wait_recv()
    kernel_sum = [[jnp.zeros((8, width), F32) for _ in range(3)] for _ in range(3)]
    for j in range(count):
        for first, r, c in segments(j):
            for m in range(members):
                mx = mx_got[m, j, first : first + seg, :].astype(F32)
                for k in range(3):
                    ahead = EDGE + 1 - k
                    wide = jnp.concatenate(
                        [
                            jnp.zeros((ahead, width), F32), mx,
                            jnp.zeros((2 * EDGE - ahead, width), F32),
                        ],
                        axis=0,
                    )
                    for i in range(3):
                        win = pad[m, 2 - i + r, c : c + seg + 2 * EDGE, :]
                        product = (wide * win).reshape(-1, 8, width)
                        kernel_sum[i][k] = kernel_sum[i][k] + jnp.sum(product, axis=0)
    s_a[core] = jnp.concatenate(
        [gain_sum]
        + [jnp.sum(kernel_sum[i][k], axis=0, keepdims=True) for i in range(3) for k in range(3)]
        + [jnp.zeros((6, width), F32)],
        axis=0,
    )
    start(push(s_a.at[core], s_a.at[core], sa_send, sa_recv, partner))
    to_rows(0)

    push(s_a.at[other], s_a.at[other], sa_send, sa_recv, partner).wait_recv()
    s_b[me_p] = s_a[0] + s_a[1]
    for p in plane_others:
        start(push(
            s_b.at[me_p], s_b.at[me_p], sb_send.at[p], sb_recv.at[me_p], plane_peer(p)
        ))
    to_rows(1)
    to_plane(0)
    for p in plane_others:
        push(s_b.at[p], s_b.at[p], sb_send.at[p], sb_recv.at[p], plane_peer(p)).wait_recv()
    s_c[row] = sum(s_b[p] for p in range(planes))
    for r in far_rows:
        start(push(s_c.at[row], s_c.at[row], sc_send.at[r], sc_recv.at[row], (mem, r, col)))
    to_plane(1)
    for o in mem_others:
        push(co_src.at[o], co_got.at[:, o], co_send.at[o], co_recv.at[o], (o, *at)).wait_recv()
    gf_ref[...] = (
        cot[...].astype(F32) + co_got[...].reshape(cot.shape).astype(F32)
    ).astype(BF16)
    from_plane(0)
    for r in row_others:
        push(s_c.at[r], s_c.at[r], sc_send.at[r], sc_recv.at[r], (mem, r, col)).wait_recv()
    small_ref[...] = sum(s_c[r] for r in range(grid_rows)) * scale
    from_plane(1)
    from_partner(0)
    from_partner(1)

    for copy in sent:
        copy.wait_send()
    for i in range(len(NEAR)):
        @pl.when(exists(NEAR[i]))
        def _():
            halo_copy(i).wait_send()
    for j in range(count):
        @pl.when(mem != j)
        def _():
            push(
                gm_src.at[:, j], gm_got.at[mem], gm_send.at[j], gm_recv.at[mem], (j, *at)
            ).wait_send()


def output_kernel(
    gf_in, out_in, small_in, gf, gain, gq, gk, gv, go, taps, taps_v, sems,
):
    copies = [
        pltpu.make_async_copy(out_in.at[i], ref, sems.at[i]) for i, ref in enumerate((gv, go, gq, gk))
    ]
    copies.append(pltpu.make_async_copy(gf_in, gf, sems.at[4]))
    copies.append(pltpu.make_async_copy(small_in.at[pl.ds(0, 1)], gain, sems.at[5]))
    for copy in copies:
        copy.start()
    for i in range(3):
        taps_v[i] = small_in[1 + 3 * i : 4 + 3 * i, :]
    last = pltpu.make_async_copy(taps_v, taps, sems.at[6])
    last.start()
    for copy in copies:
        copy.wait()
    last.wait()


def local(fields, norm_gain, w_query, w_key, w_value, w_out, mix_kernel, cotangent):
    members, rows, cols, width = fields.shape
    count, grid_rows, grid_cols = (lax.axis_size(a) for a in ("mem", "row", "col"))
    cells = rows * cols // count
    planes = count // 2 * grid_cols
    subs = 2
    unit = width // (planes * subs)
    tokens = math.prod(fields.shape[:3]) * count * grid_rows * grid_cols
    sems = pltpu.SemaphoreType.DMA
    vmem = pltpu.VMEM
    split = (members, count, cells, width)
    got = (count, members, cells, width)
    square = vmem((width, width), BF16)
    half = (2, planes, subs, unit, width)
    full = (2,) + half
    small = (16, width)
    steps = cells // BLOCK

    def pair(shape):
        return [sems(shape), sems(shape)]

    gf, out, small_sum = pl.pallas_call(
        functools.partial(
            main_kernel, (count, grid_rows, grid_cols), 1.0 / math.sqrt(tokens)
        ),
        out_shape=(
            jax.ShapeDtypeStruct(fields.shape, BF16),
            jax.ShapeDtypeStruct(full, F32),
            jax.ShapeDtypeStruct(small, F32),
        ),
        in_specs=[HBM_SPEC] * 8,
        out_specs=(VMEM_SPEC,) * 3,
        scratch_shapes=[
            vmem(fields.shape, BF16), vmem((1, width), F32), square, square, square, square,
            vmem((3, 3, width), F32),
            vmem(got, BF16), vmem(split, BF16), vmem(got, BF16), vmem(got, BF16), vmem(split, BF16),
            vmem(got, BF16), vmem(split, BF16),
            vmem((2, members, cols, width), BF16),
            vmem((2, rows, members, width), F32), vmem((2, rows + 2, members, width), F32),
            vmem((members, rows + 2, cols + 2 * EDGE, width), F32),
            vmem(full, F32), vmem(half, BF16), vmem(half, BF16), vmem(half, F32),
            vmem(half, BF16), vmem(half, BF16), vmem((2, subs, grid_rows, unit, width), BF16),
            vmem(full, BF16),
            vmem((2,) + small, F32), vmem((planes,) + small, F32), vmem((grid_rows,) + small, F32),
            sems((8,)), *pair((len(NEAR),)),
            *pair((count, steps)), *pair((count,)), *pair((count, steps)), *pair((count,)),
            *pair((2,)), *pair((2, planes, subs)), *pair((2, subs, grid_rows)),
            *pair((2, planes, subs)), *pair((2, planes, subs)),
            *pair(()), *pair((planes,)), *pair((grid_rows,)),
        ],
        compiler_params=pltpu.CompilerParams(
            collective_id=1, has_side_effects=True, vmem_limit_bytes=24 * 2**20
        ),
    )(*(
        pltpu.with_memory_space_constraint(x, pltpu.HBM)
        for x in (
            fields.reshape(split), cotangent, norm_gain.reshape(1, -1),
            w_query, w_key, w_value, w_out, mix_kernel,
        )
    ))
    square32 = jax.ShapeDtypeStruct((width, width), F32)
    gf, gain, gq, gk, gv, go, taps = pl.pallas_call(
        output_kernel,
        out_shape=(
            jax.ShapeDtypeStruct(fields.shape, BF16), jax.ShapeDtypeStruct((1, width), F32),
            square32, square32, square32, square32,
            jax.ShapeDtypeStruct((3, 3, width), F32),
        ),
        in_specs=[VMEM_SPEC] * 3,
        out_specs=(HBM_SPEC,) * 7,
        scratch_shapes=[vmem((3, 3, width), F32), sems((7,))],
        compiler_params=pltpu.CompilerParams(vmem_limit_bytes=16 * 2**20),
    )(gf, out.reshape(4, width, width), small_sum)
    return (gf, gain.reshape(-1), gq, gk, gv, go, taps)


def solution(mesh):
    tile = P("mem", "row", "col", None)
    in_specs = (tile, P(), P(), P(), P(), P(), P(), tile)
    out_specs = (tile, P(), P(), P(), P(), P(), P())
    return jax.shard_map(local, mesh=mesh, in_specs=in_specs, out_specs=out_specs, check_vma=False)
```
